256 devices in a mesh: req: 8 (over y, core), vocab: 32 (over x, z).
Axes of the slice: x: 4, y: 4, z: 8, core: 2. Of those that a mesh axis runs over, the one named last changes fastest.
Arguments:
- hidden_rows: bfloat16 [8192, 2048], P(('req', 'vocab')), may hold values from -20 to 20
- norm_gain: float32 [2048], replicated, may hold values from 0.1 to 1.9
- head_weight: bfloat16 [2048, 81920], P(None, 'vocab'), may hold values from -10 to 10
- token_ids: int32 [8192], P('req'), may hold values from 0 to 81919
- live_count: int32 [256], P(('req', 'vocab')), may hold values from 1 to 32, as said below
Outputs:
- logprob: float32 [8192], P(('req', 'vocab'))
- entropy: float32 [8192], P(('req', 'vocab'))
The draws below stay inside these ranges and needn't reach their ends.
Inputs may be any that keep to these rules, and one draw needn't show every extreme that they name: `live_count`: the live rows of an owner are its first ones; some owner has all 32 live in every draw.
All inputs are finite; a program needn't handle non-finite values.
Results may differ from the reference program's by a relative error of at most 0.012.
Values may be sent and summed in bfloat16 or wider, within the bound.
A program may use at most 64 MiB of HBM per device.

```python
import math
import jax
import jax.numpy as jnp
from jax import lax

D = 2048
VOCAB = 81920
OWN = 32
OWNERS = 256
ROWS = 8192
N_REQ = 8
N_VOCAB = 32


def aligned_columns(key):
    first_key, sign_key = jax.random.split(jax.random.fold_in(key, 7), 2)
    starts = jnp.arange(6, dtype=jnp.int32) * (VOCAB // 6)
    first = starts + jax.random.randint(first_key, (6,), 0, VOCAB // 12)
    second = first + VOCAB // 12
    target = jnp.array([120.0, 240.0, 380.0, 120.0, 240.0, 380.0], jnp.float32)
    level = target * math.sqrt(2.0) / D
    signs = (jax.random.randint(sign_key, (6, D), 0, 2) * 2 - 1).astype(jnp.float32)
    alternate = jnp.where(jnp.arange(D) % 2 == 0, 1.0, -1.0).astype(jnp.float32)
    first_vectors = signs * level[:, None]
    second_vectors = signs * alternate[None, :] * level[:, None]
    mixing = 1.0 - 2.0 / target
    return (first, second, first_vectors, second_vectors, mixing)


def draw_head_weight(key, part):
    weight_key, scale_key = jax.random.split(jax.random.fold_in(key, 1), 2)
    columns = jnp.arange(VOCAB, dtype=jnp.float32)
    scales = jnp.exp(jax.random.uniform(scale_key, (VOCAB,), jnp.float32, math.log(0.4), math.log(4.0)))
    scales = scales * (1.0 + 2.0 * columns / VOCAB)
    weight = jnp.clip(jax.random.normal(weight_key, (D, VOCAB), jnp.float32), -6.0, 6.0)
    weight = weight * D ** (-0.5) * scales[None, :]
    first, second, first_vectors, second_vectors, mixing = aligned_columns(key)
    weight = weight.at[:, first].set(first_vectors.T)
    weight = weight.at[:, second].set(second_vectors.T)
    return weight.astype(jnp.bfloat16)


def draw_hidden_rows(key, part):
    row_key = jax.random.fold_in(jax.random.fold_in(key, 2), 0)
    values = jnp.clip(jax.random.normal(row_key, (ROWS, D), jnp.float32), -6.0, 6.0)
    first, second, first_vectors, second_vectors, mixing = aligned_columns(key)
    targets = jnp.array([index * ROWS // 6 // OWN * OWN for index in range(6)], jnp.int32)
    values = values.at[targets].set(first_vectors + mixing[:, None] * second_vectors)
    return values.astype(jnp.bfloat16)


def draw_live_count(key, part):
    count_key, full_key = jax.random.split(jax.random.fold_in(key, 3), 2)
    counts = jax.random.randint(count_key, (OWNERS,), 1, OWN + 1)
    chosen = jax.random.randint(full_key, (), 0, OWNERS)
    return counts.at[chosen].set(OWN).astype(jnp.int32)


def place_ends(values, stream_key, smallest, top_value):
    longest = values.shape.index(max(values.shape))
    spots = []
    for shift in (0, 1):
        where = [jax.random.randint(jax.random.fold_in(stream_key, axis), (), 0, length) for axis, length in enumerate(values.shape)]
        where[longest] = (where[longest] + shift) % values.shape[longest]
        spots.append(tuple(where))
    return values.at[spots[0]].set(smallest).at[spots[1]].set(top_value)


def setup_inputs(seed: int = 0) -> dict:
    seeds = jax.random.split(jax.random.key(seed), 6)
    return {
        "hidden_rows": draw_hidden_rows(jax.random.fold_in(seeds[5], 71), 0),
        "norm_gain": jnp.clip(1.0 + 0.18 * jax.random.normal(seeds[1], (D,), jnp.float32), 0.1, 1.9),
        "head_weight": draw_head_weight(jax.random.fold_in(seeds[5], 71), 0),
        "token_ids": place_ends(jax.random.randint(seeds[3], (ROWS,), 0, VOCAB), jax.random.fold_in(seeds[3], 1), 0, VOCAB - 1).astype(jnp.int32),
        "live_count": draw_live_count(jax.random.fold_in(seeds[5], 71), 0),
    }


def block_stats(packed, gain, head_weight):
    block_rows, block_ids = packed
    values = block_rows.astype(jnp.float32)
    squares = lax.optimization_barrier(jnp.mean(values * values, axis=1))
    normed = (values * lax.rsqrt(squares + 1e-06)[:, None] * gain[None, :]).astype(jnp.bfloat16)
    logits = jnp.dot(normed, head_weight, preferred_element_type=jnp.float32)
    row_top = lax.optimization_barrier(jnp.max(logits, axis=1))
    shifted = logits - row_top[:, None]
    powers = jnp.exp(shifted)
    row_total = lax.optimization_barrier(jnp.sum(powers, axis=1))
    row_spread = lax.optimization_barrier(jnp.sum(powers * shifted, axis=1))
    row_picked = jnp.take_along_axis(logits, block_ids[:, None].astype(jnp.int32), axis=1)[:, 0]
    log_total = jnp.log(row_total)
    return (row_picked - row_top - log_total, log_total - row_spread / row_total)

def reference(hidden_rows, norm_gain, head_weight, token_ids, live_count):
    group_rows = OWN * N_VOCAB
    packed = (hidden_rows.reshape(N_REQ, group_rows, D), token_ids.reshape(N_REQ, group_rows))
    logprob, entropy = lax.map(lambda item: block_stats(item, norm_gain, head_weight), packed)
    logprob = logprob.reshape(-1)
    entropy = entropy.reshape(-1)
    row_index = jnp.arange(OWN * N_REQ * N_VOCAB, dtype=jnp.int32)
    limits = jnp.repeat(live_count, OWN)
    live = row_index % OWN < limits
    return (jnp.where(live, logprob, 0.0), jnp.where(live, entropy, 0.0))
```

```python
import functools

import jax
import jax.numpy as jnp
from jax import lax
from jax.experimental import pallas as pl
from jax.experimental.pallas import tpu as pltpu
from jax.sharding import PartitionSpec as P

X, Z = 4, 8
OWN = 32
HALF = 16
CHUNK = 128
PIECES = 2
GAP = 3
DIRECTIONS = ((1, 0), (-1, 0), (0, 1), (0, -1))
MESH = pl.DeviceIdType.MESH
LOWEST = -1e30

SLOTS = (
    (40, 56, 1, 39),
    (8, 24, 33, 7),
    (-1, -1, -1, -1),
    (47, 63, 2, 38),
    (9, 57, 34, 6),
    (41, 25, -1, 15),
    (10, 62, 3, 46),
    (42, 30, 35, 37),
    (55, 49, 58, 14),
    (18, 54, 11, 45),
    (50, 61, 43, 29),
    (22, 59, 36, 13),
    (53, 27, 19, 44),
    (51, 21, 12, 60),
    (23, 26, 4, 28),
    (52, 17, 20, 5),
    (48, 16, -1, 31),
)


def plan():
    arrival = {}
    transfers = {}
    for step, row in enumerate(SLOTS):
        for direction, code in enumerate(row):
            if code >= 0:
                transfers[code] = (step, direction)
                part, place = divmod(code, OWN)
                key = (part % 2, place)
                arrival[key] = max(arrival.get(key, -1), step)
    order = sorted(arrival, key=lambda key: (arrival[key], key))
    order += [(0, 0), (1, 0)]
    ready = [
        max(arrival.get(key, -1) for key in order[c : c + 8]) for c in range(0, len(order), 8)
    ]
    return transfers, order, ready


def kernel(hid, gain, tok, w_hbm, out, x, w, lg, ms, ss, ts, ps, tokt, msg, ret, w_sem, g_send, g_recv, r_send, r_recv):
    req = lax.axis_index("req")
    vocab = lax.axis_index("vocab")
    my_x, my_z = vocab // Z, vocab % Z
    width = w.shape[1]
    half = width // 2
    depth = x.shape[2]
    parts = PIECES // 2
    span = depth // parts
    transfers, order, ready = plan()
    place_of = {key: index for index, key in enumerate(order)}
    chunks = len(ready)

    def device(dx, dz):
        return (req, lax.rem(my_x + dx + X, X) * Z + lax.rem(my_z + dz + Z, Z))

    def piece_ref(code):
        part, place = divmod(code, OWN)
        chunk, index = divmod(place_of[(part % 2, place)], 8)
        return x.at[chunk, pl.ds(HALF * index, HALF), pl.ds(span * (part // 2), span)]

    weights = [
        pltpu.make_async_copy(
            w_hbm.at[:, pl.ds(half * h, half)], w.at[:, pl.ds(half * h, half)], w_sem.at[h]
        )
        for h in range(2)
    ]
    for copy in weights:
        copy.start()

    barrier = pltpu.get_barrier_semaphore()
    for dx, dz in DIRECTIONS:
        pl.semaphore_signal(barrier, inc=1, device_id=device(dx, dz), device_id_type=MESH)

    values = hid[...].astype(jnp.float32)
    squares = jnp.mean(values * values, axis=1, keepdims=True)
    normed = (values * lax.rsqrt(squares + 1e-06) * gain[...]).astype(jnp.bfloat16)
    for p in range(2):
        chunk, index = divmod(place_of[(p, 0)], 8)
        x[chunk, HALF * index : HALF * (index + 1), :] = normed[HALF * p : HALF * (p + 1), :]

    numbers = {code: n for n, code in enumerate(transfers)}
    gathers = {}
    for code, (step, direction) in transfers.items():
        part, place = divmod(code, OWN)
        dx, dz = DIRECTIONS[direction]
        source = part * OWN + (place // Z - dx) % X * Z + (place % Z - dz) % Z
        n = numbers[code]
        gathers[code] = pltpu.make_async_remote_copy(
            src_ref=piece_ref(source),
            dst_ref=piece_ref(code),
            send_sem=g_send.at[n],
            recv_sem=g_recv.at[n],
            device_id=device(dx, dz),
            device_id_type=MESH,
        )

    def send(step):
        if step < len(SLOTS):
            for code in SLOTS[step]:
                if code >= 0:
                    gathers[code].start()

    pl.semaphore_wait(barrier, len(DIRECTIONS))
    for step in range(GAP):
        send(step)

    first_col = vocab * width
    columns = (tok[...] - first_col).astype(jnp.float32)
    for g in range(tok.shape[0]):
        tokt[128 * g : 128 * (g + 1), :] = jnp.broadcast_to(columns[g : g + 1, :], (128, 128)).T

    lanes = lax.broadcasted_iota(jnp.int32, (CHUNK, 128), 1)
    lane_columns = lanes.astype(jnp.float32)
    rows = lax.broadcasted_iota(jnp.int32, (CHUNK, 128), 0)
    diagonal = lanes % HALF == rows % HALF
    segment = lanes // HALF

    def owner_of(key):
        return lax.rem(my_x - key[1] // Z + X, X) * Z + lax.rem(my_z - key[1] % Z + Z, Z)

    def dot(c, h):
        if c == 0:
            weights[h].wait()
        lg[h] = jnp.dot(
            x[c], w[:, half * h : half * (h + 1)], preferred_element_type=jnp.float32
        )

    def stats(c, h):
        keys = order[8 * c : 8 * c + 8]
        wanted = jnp.concatenate(
            [
                tokt[pl.ds(pl.multiple_of(owner_of(key) * OWN + HALF * key[0], HALF), HALF), :]
                for key in keys
            ],
            axis=0,
        )
        tiles = [lg[h, :, 128 * k : 128 * (k + 1)] for k in range(half // 128)]
        top = functools.reduce(jnp.maximum, tiles)
        if h == 0:
            total = spread = picked = jnp.zeros((CHUNK, 128), jnp.float32)
        else:
            before = ms[...]
            top = jnp.maximum(before, top)
            moved = before - top
            factor = jnp.exp(moved)
            total = ss[...]
            spread = (ts[...] + moved * total) * factor
            total = total * factor
            picked = ps[...]
        for k, tile in enumerate(tiles):
            shifted = tile - top
            power = jnp.exp(shifted)
            total = total + power
            spread = spread + power * shifted
            picked = jnp.where(wanted - (half * h + 128 * k) == lane_columns, tile, picked)
        if h == 0:
            ms[...], ss[...], ts[...], ps[...] = top, total, spread, picked
            return
        row_top = jnp.max(top, axis=1, keepdims=True)
        moved = top - row_top
        factor = jnp.exp(moved)
        row_spread = jnp.sum((spread + moved * total) * factor, axis=1, keepdims=True)
        row_total = jnp.sum(total * factor, axis=1, keepdims=True)
        row_picked = jnp.sum(picked, axis=1, keepdims=True)
        packed = jnp.where(
            segment >= 4,
            row_top,
            jnp.where(segment == 1, row_spread, jnp.where(segment == 2, row_picked, row_total)),
        )
        packed = jnp.where(diagonal, packed, 0.0)
        for i, key in enumerate(keys):
            line = jnp.sum(packed[HALF * i : HALF * (i + 1)], axis=0, keepdims=True)
            if key[1] == 0:
                ret[key[0] * OWN] = line
            else:
                msg[8 * c + i] = line
        for i, key in enumerate(keys):
            if key[1] != 0:
                returns[key].start()

    returns = {}
    for index, key in enumerate(order):
        if key[1] != 0:
            n = key[0] * OWN + key[1]
            returns[key] = pltpu.make_async_remote_copy(
                src_ref=msg.at[index],
                dst_ref=ret.at[n],
                send_sem=r_send.at[n],
                recv_sem=r_recv.at[n],
                device_id=device(-(key[1] // Z), -(key[1] % Z)),
                device_id_type=MESH,
            )

    steps = [(c, h) for c in range(chunks) for h in range(2)]
    done = 0

    def compute():
        nonlocal done
        dot(*steps[done])
        if done:
            stats(*steps[done - 1])
        done += 1

    for step, row in enumerate(SLOTS):
        for code in row:
            if code >= 0:
                gathers[code].wait_recv()
        send(step + GAP)
        if step % parts == parts - 1 and ready[steps[done][0]] <= step:
            compute()
    while done < len(steps):
        compute()
    stats(*steps[-1])

    for copy in gathers.values():
        copy.wait_send()
    for copy in returns.values():
        copy.wait_send()
    for copy in returns.values():
        copy.wait_recv()

    lane = lax.broadcasted_iota(jnp.int32, (1, 128), 1)
    seg = lane // HALF
    results = []
    for p in range(2):
        lines = [ret[p * OWN + i] for i in range(OWN)]
        tops = [pltpu.roll(line, 64, 1) for line in lines]
        top = functools.reduce(jnp.maximum, tops)
        sums = jnp.zeros((1, 128), jnp.float32)
        for line, shard_top in zip(lines, tops):
            moved = shard_top - top
            factor = jnp.where(seg == 2, 1.0, jnp.exp(moved))
            factor = jnp.where(seg == 3, factor * moved, factor)
            sums = sums + line * factor
        spread = pltpu.roll(sums, 112, 1) + pltpu.roll(sums, 80, 1)
        picked = pltpu.roll(sums, 96, 1)
        log_total = jnp.log(sums)
        results.append((picked - top - log_total, log_total - spread / sums))
    for i in range(2):
        second = pltpu.roll(results[1][i], HALF, 1)
        out[i : i + 1, :] = jnp.where(lane < HALF, results[0][i], second)


def per_device(hidden_rows, norm_gain, head_weight, token_ids, live_count):
    own, depth = hidden_rows.shape
    width = head_weight.shape[1]
    group = token_ids.shape[0]
    vmem = pl.BlockSpec(memory_space=pltpu.VMEM)
    stat = pltpu.VMEM((CHUNK, 128), jnp.float32)
    result = pl.pallas_call(
        kernel,
        out_shape=jax.ShapeDtypeStruct((2, 128), jnp.float32),
        in_specs=[vmem, vmem, vmem, pl.BlockSpec(memory_space=pl.ANY)],
        out_specs=vmem,
        scratch_shapes=[
            pltpu.VMEM((group // CHUNK, CHUNK, depth), jnp.bfloat16),
            pltpu.VMEM((depth, width), jnp.bfloat16),
            pltpu.VMEM((2, CHUNK, width // 2), jnp.float32),
            stat,
            stat,
            stat,
            stat,
            pltpu.VMEM((group, 128), jnp.float32),
            pltpu.VMEM((2 * OWN, 1, 128), jnp.float32),
            pltpu.VMEM((2 * OWN, 1, 128), jnp.float32),
            pltpu.SemaphoreType.DMA((2,)),
            pltpu.SemaphoreType.DMA((PIECES * (OWN - 1),)),
            pltpu.SemaphoreType.DMA((PIECES * (OWN - 1),)),
            pltpu.SemaphoreType.DMA((2 * OWN,)),
            pltpu.SemaphoreType.DMA((2 * OWN,)),
        ],
        compiler_params=pltpu.CompilerParams(
            collective_id=0, has_side_effects=True, vmem_limit_bytes=56 << 20
        ),
        name="head_stats",
    )(hidden_rows, norm_gain.reshape(1, depth), token_ids.reshape(group // 128, 128), head_weight)
    live = jnp.arange(own, dtype=jnp.int32) < live_count[0]
    return (
        jnp.where(live, result[0, :own], 0.0),
        jnp.where(live, result[1, :own], 0.0),
    )


def solution(mesh):
    placed = (P(("req", "vocab"), None), P(), P(None, "vocab"), P("req"), P(("req", "vocab")))
    return jax.shard_map(
        per_device,
        mesh=mesh,
        in_specs=placed,
        out_specs=(P(("req", "vocab")), P(("req", "vocab"))),
        check_vma=False,
    )
```
